32 devices in a mesh: group: 2 (over y), scan: 4 (over z), tensor: 2 (over x), band: 2 (over core).
Axes of the slice: x: 2, y: 2, z: 4, core: 2. Of those that a mesh axis runs over, the one named last changes fastest.
Arguments:
- signal: bfloat16 [4096, 5120], P(('group', 'scan', 'band'), 'tensor'), parts along dimension 0, may hold values from -140 to 140
- gate_branch: bfloat16 [4096, 5120], P(('group', 'scan', 'band'), 'tensor'), parts along dimension 0, may hold values from -6 to 6
- write_proj: bfloat16 [4096, 128], P(('group', 'scan', 'band')), parts along dimension 0, may hold values from -1.796875 to 1.796875
- read_proj: bfloat16 [4096, 128], P(('group', 'scan', 'band')), parts along dimension 0, may hold values from -1.796875 to 1.796875
- step_logits: float32 [80, 4096], P('tensor', ('group', 'scan', 'band')), parts along dimension 1
- valid_mask: int32 [4096], P(('group', 'scan', 'band')), parts along dimension 0, may hold values from 0 to 1
- stretch_band: int32 [16], P(('group', 'scan', 'band')), parts along dimension 0, may hold values from 0 to 11
- band_offset: float32 [12, 80], P(None, 'tensor'), may hold values from -0.35 to 0.35
- decay_log: float32 [80], P('tensor'), may hold values from -8 to 0
- step_offset: float32 [80], P('tensor'), may hold values from -7 to -1
- skip_gain: float32 [80], P('tensor'), may hold values from 0.5 to 2
- norm_gain: float32 [5120], P('tensor'), may hold values from 0.1 to 1.9
- out_weight: bfloat16 [5120, 2560], P('tensor'), may hold values from -0.078125 to 0.078125
Outputs:
- layer_output: bfloat16 [4096, 2560], P(('group', 'scan', 'band'), 'tensor'), parts along dimension 0
The draws below stay inside these ranges and needn't reach their ends.
There are 2 independent parts, one for each index of `group`. The reference program is written for one: setup_inputs(seed, part) draws one part's arguments, and reference() takes and returns one part's arrays. A program takes and returns all parts, laid end to end along the dimension named above; an argument that names none is the same for every part. Nothing has to cross between parts.
All inputs are finite; a program needn't handle non-finite values.
Results may differ from the reference program's by a relative error of at most 0.015.
Values may be sent and summed in bfloat16 or wider, within the bound.
A program may use at most 64 MiB of HBM per device.

```python
import math
import jax
import jax.numpy as jnp
from jax import lax

WIDTH = 2560
HEADS = 80
HEAD_DIM = 64
STATE = 128
STRETCH = 256
BANDS = 12
SEQUENCE_LENGTH = 2048
STRETCHES = 8
INNER = 5120
N_TENSOR = 2


def head_params(key):
    slow_share = 0.5
    chooser = jax.random.uniform(jax.random.fold_in(key, 101), (HEADS,))
    initial_sample = jax.random.uniform(jax.random.fold_in(key, 102), (HEADS,))
    second_draw = jax.random.uniform(jax.random.fold_in(key, 103), (HEADS,))
    root_length = jnp.sqrt(jnp.float32(SEQUENCE_LENGTH))
    slow_step = 0.5 * jnp.exp(initial_sample * jnp.log(4.0)) / root_length
    slow_rate = 0.3 * jnp.exp(second_draw * jnp.log(2.0)) / root_length
    fast_step = 0.1 * jnp.exp(initial_sample * jnp.log(2.0))
    fast_rate = jnp.exp(jnp.log(1.0 / 50.0) + second_draw * jnp.log(50.0 / 30.0)) / fast_step
    is_slow = chooser < slow_share
    return (jnp.where(is_slow, slow_step, fast_step), jnp.where(is_slow, slow_rate, fast_rate))


def spike_indices(key):
    return jax.random.randint(jax.random.fold_in(key, 211), (2,), 0, SEQUENCE_LENGTH)


def draw_decay_log(key, part):
    return jnp.log(head_params(key)[1])


def draw_step_offset(key, part):
    return jnp.log(jnp.expm1(head_params(key)[0]))


def draw_valid_mask(key, part):
    coin_outcome = jax.random.randint(jax.random.fold_in(key, 212), (SEQUENCE_LENGTH,), 0, 4)
    sample_places = spike_indices(key)
    spike_indicator = jnp.any(jnp.arange(SEQUENCE_LENGTH, dtype=jnp.int32)[:, None] == sample_places[None, :], axis=1)
    return jnp.where(spike_indicator | (coin_outcome == 0), 0, 1).astype(jnp.int32)


def draw_step_logits(key, part):
    rough_part = jax.random.uniform(jax.random.fold_in(key, 213), (HEADS, SEQUENCE_LENGTH), minval=-0.7, maxval=0.7)
    intensity = jax.random.uniform(jax.random.fold_in(key, 214), (2,), minval=0.8, maxval=1.1) * jnp.sqrt(jnp.float32(SEQUENCE_LENGTH))
    sample_places = spike_indices(key)
    boost = jnp.sum(jnp.where(jnp.arange(SEQUENCE_LENGTH, dtype=jnp.int32)[:, None] == sample_places[None, :], intensity[None, :], 0.0), axis=1)
    return rough_part + boost[None, :]


def draw_signal(key, part):
    row_scale = jnp.exp(jax.random.uniform(jax.random.fold_in(key, 301), (SEQUENCE_LENGTH, 1)) * jnp.log(10.0))
    column_scale = jnp.exp(jax.random.uniform(jax.random.fold_in(key, 302), (1, INNER)) * jnp.log(10.0))
    ramp_power = 0.5
    slope_scale = jnp.exp(ramp_power * jnp.log(3.0) * jnp.arange(INNER, dtype=jnp.float32)[None, :] / (INNER - 1))
    noise_part = jnp.clip(jax.random.normal(jax.random.fold_in(key, 303), (SEQUENCE_LENGTH, INNER)), -4.0, 4.0)
    return (0.2 * noise_part * row_scale * column_scale * slope_scale).astype(jnp.bfloat16)


def plant(values, rng, least, largest):
    longest = values.shape.index(max(values.shape))
    spots = []
    for shift in (0, 1):
        where = [jax.random.randint(jax.random.fold_in(rng, axis), (), 0, length) for axis, length in enumerate(values.shape)]
        where[longest] = (where[longest] + shift) % values.shape[longest]
        spots.append(tuple(where))
    return values.at[spots[0]].set(least).at[spots[1]].set(largest)


def level_of(key, extent, split, low, high):
    loudness, own = 1.0, jax.random.fold_in(key, 6)
    for dim, shards_of in split:
        draws = jnp.exp(jax.random.uniform(jax.random.fold_in(own, dim), (shards_of,), jnp.float32, low / len(split), high / len(split)))
        loudness = loudness * jnp.repeat(draws, extent[dim] // shards_of).reshape([-1 if axis == dim else 1 for axis in range(len(extent))])
    return loudness


def noise(stream_key, shape, scale, most, cuts=(), kind=jnp.bfloat16):
    values = scale * jax.random.normal(stream_key, shape, jnp.float32)
    if cuts:
        values = values * level_of(stream_key, shape, cuts, -0.22, 0.18)
    return jnp.clip(values, -most, most).astype(kind)


def setup_inputs(seed: int = 0, part: int = 0) -> dict:
    arg_keys = jax.random.split(jax.random.key(seed), 14)
    part_keys = jax.random.split(jax.random.fold_in(arg_keys[13], part), 14)
    return {
        "signal": draw_signal(jax.random.fold_in(jax.random.fold_in(arg_keys[13], part), 71), part),
        "gate_branch": noise(part_keys[1], (SEQUENCE_LENGTH, INNER), 1.0, 6.0, ((0, 8), (1, 2))),
        "write_proj": noise(part_keys[2], (SEQUENCE_LENGTH, STATE), 0.3, 1.796875, ((0, 8),)),
        "read_proj": noise(part_keys[3], (SEQUENCE_LENGTH, STATE), 0.3, 1.796875, ((0, 8),)),
        "step_logits": draw_step_logits(jax.random.fold_in(jax.random.fold_in(arg_keys[13], part), 71), part),
        "valid_mask": draw_valid_mask(jax.random.fold_in(jax.random.fold_in(arg_keys[13], part), 71), part),
        "stretch_band": plant(jax.random.randint(part_keys[6], (STRETCHES,), 0, BANDS), jax.random.fold_in(part_keys[6], 1), 0, BANDS - 1).astype(jnp.int32),
        "band_offset": jnp.clip(jax.random.uniform(arg_keys[7], (BANDS, HEADS), jnp.float32, -0.35, 0.35) * level_of(arg_keys[7], (BANDS, HEADS), ((1, 2),), -0.4, 0.0), -0.35, 0.35),
        "decay_log": draw_decay_log(jax.random.fold_in(arg_keys[13], 71), part),
        "step_offset": draw_step_offset(jax.random.fold_in(arg_keys[13], 71), part),
        "skip_gain": jnp.clip(jnp.exp(math.log(2.0) - 1.3862944 * jax.random.uniform(arg_keys[10], (HEADS,), jnp.float32) ** level_of(arg_keys[10], (HEADS,), ((0, 2),), -0.2, 0.2)), 0.5, 2.0),
        "norm_gain": jnp.clip(1.0 + 0.18 * jax.random.normal(arg_keys[11], (INNER,), jnp.float32), 0.1, 1.9),
        "out_weight": noise(arg_keys[12], (INNER, WIDTH), INNER ** -0.5, 0.078125, ((0, 2),)),
    }


EPSILON = 1e-05

def step_sizes(step_logits, stretch_band, band_offset, step_offset):
    one_hot = (stretch_band[:, None] == jnp.arange(BANDS, dtype=jnp.int32)[None, :]).astype(jnp.float32)
    stretch_offset = jnp.dot(one_hot, band_offset, precision=lax.Precision.HIGHEST)
    token_offset = jnp.repeat(stretch_offset, STRETCH, axis=0).T
    return jax.nn.softplus(step_logits + step_offset[:, None] + token_offset)

def split_state(state):
    state_high = state.astype(jnp.bfloat16)
    widened = lax.optimization_barrier(state_high).astype(jnp.float32)
    state_low = (state - widened).astype(jnp.bfloat16)
    return (state_high, state_low)

def stretch_pass(carry_state, pieces):
    signal_block, write_block, read_block, segment_damping, weight_block = pieces
    running = jnp.cumsum(segment_damping, axis=1)
    scores = jnp.dot(read_block, write_block.T, preferred_element_type=jnp.float32)
    lower_mask = jnp.arange(STRETCH)[:, None] >= jnp.arange(STRETCH)[None, :]
    span_logs = jnp.where(lower_mask[None], running[:, :, None] - running[:, None, :], -1e+30)
    mixing = (jnp.exp(span_logs) * scores[None] * weight_block[:, None, :]).astype(jnp.bfloat16)
    local_out = jnp.einsum('hij,jhp->ihp', mixing.astype(jnp.float32), signal_block.astype(jnp.float32), precision=lax.Precision.HIGHEST)
    state_high, state_low = split_state(carry_state)
    read_wide = read_block.astype(jnp.float32)
    high_part = jnp.einsum('in,hpn->ihp', read_wide, state_high.astype(jnp.float32), precision=lax.Precision.HIGHEST)
    low_part = jnp.einsum('in,hpn->ihp', read_wide, state_low.astype(jnp.float32), precision=lax.Precision.HIGHEST)
    carried_out = jnp.exp(running).T[:, :, None] * (high_part + low_part)
    tail_weight = jnp.exp(running[:, -1:] - running) * weight_block
    scaled = (signal_block.astype(jnp.float32) * tail_weight.T[:, :, None]).astype(jnp.bfloat16)
    stretch_state = jnp.einsum('jhp,jn->hpn', scaled.astype(jnp.float32), write_block.astype(jnp.float32), precision=lax.Precision.HIGHEST)
    next_state = jnp.exp(running[:, -1])[:, None, None] * carry_state + stretch_state
    return (next_state, local_out + carried_out)

def reference(signal, gate_branch, write_proj, read_proj, step_logits, valid_mask, stretch_band, band_offset, decay_log, step_offset, skip_gain, norm_gain, out_weight):
    step_size = step_sizes(step_logits, stretch_band, band_offset, step_offset)
    log_decay = step_size * (-jnp.exp(decay_log))[:, None]
    input_weight = step_size * valid_mask.astype(jnp.float32)[None, :]
    stretch_count = SEQUENCE_LENGTH // STRETCH
    signal_blocks = signal.reshape(stretch_count, STRETCH, HEADS, HEAD_DIM)
    write_blocks = write_proj.reshape(stretch_count, STRETCH, STATE)
    read_blocks = read_proj.reshape(stretch_count, STRETCH, STATE)
    decay_blocks = log_decay.reshape(HEADS, stretch_count, STRETCH).transpose(1, 0, 2)
    weight_blocks = input_weight.reshape(HEADS, stretch_count, STRETCH).transpose(1, 0, 2)
    start_state = jnp.zeros((HEADS, HEAD_DIM, STATE), jnp.float32)
    final_state, outputs = lax.scan(stretch_pass, start_state, (signal_blocks, write_blocks, read_blocks, decay_blocks, weight_blocks))
    ssm_out = outputs.reshape(SEQUENCE_LENGTH, HEADS, HEAD_DIM) + skip_gain[None, :, None] * signal.reshape(SEQUENCE_LENGTH, HEADS, HEAD_DIM).astype(jnp.float32)
    gated_out = ssm_out.reshape(SEQUENCE_LENGTH, INNER) * jax.nn.silu(gate_branch.astype(jnp.float32))
    mean_square = lax.optimization_barrier(jnp.mean(gated_out * gated_out, axis=1, keepdims=True))
    normed = (gated_out * lax.rsqrt(mean_square + EPSILON) * norm_gain[None, :]).astype(jnp.bfloat16)
    slice_width = INNER // N_TENSOR
    summed = jnp.zeros((SEQUENCE_LENGTH, WIDTH), jnp.float32)
    for member in range(N_TENSOR):
        partial_sum = jnp.dot(normed[:, member * slice_width:(member + 1) * slice_width], out_weight[member * slice_width:(member + 1) * slice_width], preferred_element_type=jnp.float32).astype(jnp.bfloat16)
        partial_sum = lax.optimization_barrier(partial_sum)
        summed = summed + partial_sum.astype(jnp.float32)
    return summed.astype(jnp.bfloat16)
```

```python
import functools

import jax
import jax.numpy as jnp
from jax import lax
from jax.experimental import pallas as pl
from jax.experimental.pallas import tpu as pltpu
from jax.sharding import PartitionSpec as P

HEAD_DIM = 64
STATE = 128
STRETCH = 256
BANDS = 12
INNER = 5120


EPSILON = 1e-05
HIGHEST = lax.Precision.HIGHEST


def step_sizes(step_logits, stretch_band, band_offset, step_offset):
    one_hot = (stretch_band[:, None] == jnp.arange(BANDS, dtype=jnp.int32)[None, :]).astype(
        jnp.float32
    )
    stretch_offset = jnp.dot(one_hot, band_offset, precision=HIGHEST)
    token_offset = jnp.repeat(stretch_offset, STRETCH, axis=0).T
    return jax.nn.softplus(step_logits + step_offset[:, None] + token_offset)


def combine(earlier, later_pair):
    return (
        earlier[0] + later_pair[0],
        jnp.exp(later_pair[0])[:, None, None] * earlier[1] + later_pair[1],
    )


def local_step(running_pair, member):
    return (combine(running_pair, member), running_pair)


def on_device(
    signal,
    gate_branch,
    write_proj,
    read_proj,
    step_logits,
    valid_mask,
    stretch_band,
    band_offset,
    decay_log,
    step_offset,
    skip_gain,
    norm_gain,
    out_weight,
):
    row_count = signal.shape[0]
    head_count = decay_log.shape[0]
    block_count = row_count // STRETCH
    step_size = step_sizes(step_logits, stretch_band, band_offset, step_offset)
    log_decay = step_size * (-jnp.exp(decay_log))[:, None]
    input_weight = step_size * valid_mask.astype(jnp.float32)[None, :]
    running = jnp.cumsum(log_decay.reshape(head_count, block_count, STRETCH), axis=2)
    weight_blocks = input_weight.reshape(head_count, block_count, STRETCH)
    signal_blocks = signal.reshape(block_count, STRETCH, head_count, HEAD_DIM)
    write_blocks = write_proj.reshape(block_count, STRETCH, STATE)
    read_blocks = read_proj.reshape(block_count, STRETCH, STATE)
    scores = jnp.einsum(
        "cin,cjn->cij", read_blocks, write_blocks, preferred_element_type=jnp.float32
    )
    lower_mask = jnp.arange(STRETCH)[:, None] >= jnp.arange(STRETCH)[None, :]
    span_logs = jnp.where(
        lower_mask[None, None], running[:, :, :, None] - running[:, :, None, :], -1e30
    )
    mixing = (jnp.exp(span_logs) * scores[None] * weight_blocks[:, :, None, :]).astype(jnp.bfloat16)
    local_out = jnp.einsum(
        "hcij,cjhp->cihp", mixing, signal_blocks, preferred_element_type=jnp.float32
    )
    tail_weight = jnp.exp(running[:, :, -1:] - running) * weight_blocks
    scaled = (
        signal_blocks.astype(jnp.float32) * jnp.transpose(tail_weight, (1, 2, 0))[:, :, :, None]
    ).astype(jnp.bfloat16)
    block_states = jnp.einsum(
        "cjhp,cjn->chpn", scaled, write_blocks, preferred_element_type=jnp.float32
    )
    block_decay = running[:, :, -1].T
    zero_state = jnp.zeros((head_count, HEAD_DIM, STATE), jnp.float32)
    zero_log = jnp.zeros((head_count,), jnp.float32)
    identity = (zero_log, zero_state)
    device_pair, segment_cumulative = lax.scan(local_step, identity, (block_decay, block_states))
    all_logs = lax.all_gather(device_pair[0][None], ("scan", "band"), axis=0, tiled=True)
    inclusive = jnp.cumsum(all_logs, axis=0)
    exclusive = inclusive - all_logs
    position = lax.axis_index(("scan", "band"))
    own_exclusive = lax.dynamic_index_in_dim(exclusive, position, 0, keepdims=False)
    shard_block = lax.all_gather(
        device_pair[1][None].astype(jnp.bfloat16), ("scan", "band"), axis=0, tiled=True
    ).astype(jnp.float32)
    how_many = shard_block.shape[0]
    sources = jnp.arange(how_many, dtype=jnp.int32)
    gap_logs = jnp.where((sources < position)[:, None], own_exclusive[None, :] - inclusive, -1e30)
    carry_state = zero_state + jnp.einsum(
        "kh,khpn->hpn", jnp.exp(gap_logs), shard_block, precision=HIGHEST
    )
    enter_state = (
        jnp.exp(segment_cumulative[0])[:, :, None, None] * carry_state[None] + segment_cumulative[1]
    )
    state_high = enter_state.astype(jnp.bfloat16)
    widened = lax.optimization_barrier(state_high).astype(jnp.float32)
    state_low = (enter_state - widened).astype(jnp.bfloat16)
    high_part = jnp.einsum(
        "cin,chpn->cihp", read_blocks, state_high, preferred_element_type=jnp.float32
    )
    low_part = jnp.einsum(
        "cin,chpn->cihp", read_blocks, state_low, preferred_element_type=jnp.float32
    )
    carried_out = jnp.transpose(jnp.exp(running), (1, 2, 0))[:, :, :, None] * (high_part + low_part)
    ssm_out = (local_out + carried_out).reshape(row_count, head_count, HEAD_DIM) + skip_gain[
        None, :, None
    ] * signal.reshape(row_count, head_count, HEAD_DIM).astype(jnp.float32)
    gated_out = ssm_out.reshape(row_count, head_count * HEAD_DIM) * jax.nn.silu(
        gate_branch.astype(jnp.float32)
    )
    square_total = lax.psum(jnp.sum(gated_out * gated_out, axis=1), "tensor")
    normed = (
        gated_out * lax.rsqrt(square_total / INNER + EPSILON)[:, None] * norm_gain[None, :]
    ).astype(jnp.bfloat16)
    own_columns = lax.psum_scatter(
        lax.dot_general(
            out_weight, normed, (((0,), (1,)), ((), ())), preferred_element_type=jnp.float32
        ).astype(jnp.bfloat16),
        "tensor",
        scatter_dimension=0,
        tiled=True,
    ).astype(jnp.float32)
    return own_columns.T.astype(jnp.bfloat16)


LOG2E = 1.4426950408889634
LANES = 128
PAIRS = 2
TILE = 256
MESH = pl.DeviceIdType.MESH


def fused_kernel(
    heads,
    span_count,
    band_count,
    signal_ref,
    gate_hbm,
    write_ref,
    read_ref,
    logits_ref,
    valid_ref,
    band_ref,
    offset_ref,
    decay_ref,
    bias_ref,
    skip_ref,
    gain_ref,
    weight_hbm,
    out_ref,
    weight_ref,
    gate_ref,
    padded_ref,
    params_ref,
    row_ref,
    spread_ref,
    skip_rows_ref,
    scores_ref,
    read_by_token_ref,
    run_ref,
    lead_ref,
    fed_ref,
    state_ref,
    total_ref,
    local_ref,
    normed_ref,
    square_ref,
    carry_ref,
    pass_ref,
    sent_ref,
    landed_ref,
    square_out_ref,
    square_in_ref,
    load_sem,
    chain_send,
    chain_recv,
    tile_send,
    tile_recv,
    square_send,
    square_recv,
):
    pair_count = heads // 2
    chunk_count = pair_count // PAIRS
    places = span_count * band_count
    scan_index = lax.axis_index("scan")
    band_index = lax.axis_index("band")
    tensor_index = lax.axis_index("tensor")
    place = scan_index * band_count + band_index
    following = lax.rem(place + 1, places)
    previous = lax.rem(place + places - 1, places)
    peer = 1 - tensor_index

    def at_place(spot):
        return {"scan": spot // band_count, "band": lax.rem(spot, band_count)}

    barrier = pltpu.get_barrier_semaphore()
    for target in (at_place(following), at_place(previous), {"tensor": peer}):
        pl.semaphore_signal(barrier, inc=1, device_id=target, device_id_type=MESH)
    gate_load = pltpu.make_async_copy(gate_hbm, gate_ref, load_sem.at[0])
    weight_load = pltpu.make_async_copy(weight_hbm, weight_ref, load_sem.at[1])
    gate_load.start()
    weight_load.start()

    padded_ref[...] = jnp.zeros_like(padded_ref)
    padded_ref[0:heads, :] = logits_ref[...]
    params_ref[...] = jnp.zeros_like(params_ref)
    chosen = lax.broadcasted_iota(jnp.int32, (BANDS, heads), 0) == band_ref[0]
    params_ref[0:1, 0:heads] = bias_ref[...] + jnp.sum(
        jnp.where(chosen, offset_ref[...], 0.0), axis=0, keepdims=True
    )
    params_ref[1:2, 0:heads] = jnp.exp(decay_ref[...])
    params_ref[2:3, 0:heads] = skip_ref[...]
    shifted = padded_ref[...].T + params_ref[0:1, :]
    step_size = jnp.maximum(shifted, 0.0) + jnp.log1p(jnp.exp(-jnp.abs(shifted)))
    lanes = lax.broadcasted_iota(jnp.int32, (STRETCH, LANES), 1)
    tokens = lax.broadcasted_iota(jnp.int32, (STRETCH, LANES), 0)
    real = lanes < heads
    running = jnp.where(real, step_size * -params_ref[1:2, :], 0.0)
    shift = 1
    while shift < STRETCH:
        running = running + jnp.where(tokens >= shift, pltpu.roll(running, shift, 0), 0.0)
        shift *= 2
    running = running * LOG2E
    row_ref[...] = running.T
    valid = jnp.broadcast_to(valid_ref[...].astype(jnp.float32), (LANES, STRETCH)).T
    in_weight = jnp.where(real, step_size * valid, 0.0)

    def three_parts(value):
        high = value.astype(jnp.bfloat16).astype(jnp.float32)
        rest = value - high
        middle = rest.astype(jnp.bfloat16).astype(jnp.float32)
        low = rest - middle
        packed = high + pltpu.roll(middle, heads, 1) + pltpu.roll(low, 2 * heads, 1)
        return packed.astype(jnp.bfloat16)

    spread_ref[:, 0:LANES] = three_parts(running)
    spread_ref[:, LANES : 2 * LANES] = three_parts(in_weight)
    skip_rows_ref[...] = three_parts(jnp.broadcast_to(params_ref[2:3, :], (16, LANES)))
    write_turned = write_ref[...].astype(jnp.float32).T.astype(jnp.bfloat16)
    read_by_token_ref[...] = write_turned
    scores = jnp.dot(read_ref[...], write_turned, preferred_element_type=jnp.float32)
    square_rows = lax.broadcasted_iota(jnp.int32, (STRETCH, STRETCH), 0)
    square_columns = lax.broadcasted_iota(jnp.int32, (STRETCH, STRETCH), 1)
    scores_ref[...] = jnp.where(square_columns <= square_rows, scores, 0.0)
    square_ref[...] = jnp.zeros_like(square_ref)

    @pl.when(place == 0)
    def _():
        carry_ref[...] = jnp.zeros_like(carry_ref)

    pl.semaphore_wait(barrier, 3)

    def chain_copy(chunk):
        return pltpu.make_async_remote_copy(
            src_ref=pass_ref.at[chunk],
            dst_ref=carry_ref.at[chunk],
            send_sem=chain_send.at[chunk],
            recv_sem=chain_recv.at[chunk],
            device_id=at_place(following),
            device_id_type=MESH,
        )

    def chain_step(chunk):
        @pl.when(place > 0)
        def _():
            chain_copy(chunk).wait_recv()

        @pl.when(place < places - 1)
        def _():
            for member in range(PAIRS):
                pair = chunk * PAIRS + member
                onward = (
                    total_ref[pair][0:1, :] * carry_ref[chunk, member].astype(jnp.float32)
                    + state_ref[pair]
                )
                pass_ref[chunk, member] = onward.astype(jnp.bfloat16)
            chain_copy(chunk).start()

    def columns_of(pair):
        return pl.ds(pl.multiple_of(pair * LANES, LANES), LANES)

    part = lax.broadcasted_iota(jnp.int32, (LANES, 2 * LANES), 0)
    part = (
        part
        - jnp.where(part >= heads, heads, 0)
        - jnp.where(part >= 2 * heads, heads, 0)
    )
    wide_side = lax.broadcasted_iota(jnp.int32, (LANES, 2 * LANES), 1) // LANES
    wide_index = part - wide_side
    narrow_side = lax.broadcasted_iota(jnp.int32, (LANES, LANES), 1) // HEAD_DIM
    narrow_index = part[:, 0:LANES] - narrow_side
    first_half = lanes < HEAD_DIM

    def picker(index, pair):
        return jnp.where(index == 2 * pair, 1.0, 0.0).astype(jnp.bfloat16)

    def state_pair(pair):
        columns = columns_of(pair)
        both = jnp.dot(
            spread_ref[:, 0:LANES], picker(wide_index, pair), preferred_element_type=jnp.float32
        )
        run_ref[pair] = both
        weight = jnp.dot(
            spread_ref[:, LANES : 2 * LANES],
            picker(narrow_index, pair),
            preferred_element_type=jnp.float32,
        )
        own_run = jnp.where(first_half, both[:, 0:LANES], both[:, LANES : 2 * LANES])
        last_run = own_run[STRETCH - 1 : STRETCH, :]
        fed = signal_ref[:, columns].astype(jnp.float32) * weight
        fed_ref[:, columns] = fed.astype(jnp.bfloat16)
        lead_ref[:, columns] = jnp.exp2(own_run)
        scaled = (fed * jnp.exp2(last_run - own_run)).astype(jnp.bfloat16)
        state_ref[pair] = jnp.dot(
            read_by_token_ref[...], scaled, preferred_element_type=jnp.float32
        )
        total_ref[pair] = jnp.broadcast_to(jnp.exp2(last_run), (8, LANES))

    def mix_pair(pair):
        columns = columns_of(pair)
        half = STRETCH // 2
        tops, bottoms = [], []
        fed = fed_ref[:, columns]
        for side in range(2):
            row = row_ref[pl.ds(2 * pair + side, 1), :]
            run = run_ref[pair, :, side * LANES : (side + 1) * LANES]
            near = jnp.exp2(jnp.minimum(run[0:half] - row[:, 0:half], 0.0))
            far = jnp.exp2(jnp.minimum(run[half:] - row[:, 0:half], 0.0))
            late = jnp.exp2(jnp.minimum(run[half:] - row[:, half:], 0.0))
            near = (near * scores_ref[0:half, 0:half]).astype(jnp.bfloat16)
            far = (far * scores_ref[half:, 0:half]).astype(jnp.bfloat16)
            late = (late * scores_ref[half:, half:]).astype(jnp.bfloat16)
            tops.append(jnp.dot(near, fed[0:half], preferred_element_type=jnp.float32))
            bottoms.append(
                jnp.dot(
                    jnp.concatenate([far, late], axis=1), fed, preferred_element_type=jnp.float32
                )
            )
        local_ref[0:half, columns] = jnp.where(first_half[0:half], tops[0], tops[1])
        local_ref[half:, columns] = jnp.where(first_half[half:], bottoms[0], bottoms[1])

    def gate_pair(chunk, member):
        pair = chunk * PAIRS + member
        columns = columns_of(pair)
        carried = jnp.dot(
            read_ref[...], carry_ref[chunk, member], preferred_element_type=jnp.float32
        )
        skip = jnp.dot(
            skip_rows_ref[...], picker(narrow_index, pair), preferred_element_type=jnp.float32
        )
        ssm_out = (
            local_ref[:, columns]
            + lead_ref[:, columns] * carried
            + skip[0:1, :] * signal_ref[:, columns].astype(jnp.float32)
        )
        gate = gate_ref[:, columns].astype(jnp.float32)
        gated = ssm_out * (gate / (1.0 + jnp.exp(-gate)))
        square_ref[...] += gated * gated
        normed_ref[:, columns] = (gated * gain_ref[:, columns]).astype(jnp.bfloat16)

    @pl.loop(0, chunk_count)
    def _(chunk):
        for member in range(PAIRS):
            state_pair(chunk * PAIRS + member)

        @pl.when(place == 0)
        def _():
            chain_step(chunk)

    delay = jnp.minimum(chunk_count, (place * 3) // 2)

    def chain_slot(slot):
        chunk = slot - delay

        @pl.when((place > 0) & (chunk >= 0) & (chunk < chunk_count))
        def _():
            chain_step(chunk)

    @pl.loop(0, chunk_count)
    def _(slot):
        chain_slot(slot)
        for member in range(PAIRS):
            mix_pair(slot * PAIRS + member)

    gate_load.wait()

    @pl.loop(0, chunk_count)
    def _(slot):
        chain_slot(slot + chunk_count)
        for member in range(PAIRS):
            gate_pair(slot, member)

    square_sum = jnp.sum(square_ref[...].T, axis=0, keepdims=True)
    square_out_ref[...] = jnp.broadcast_to(square_sum, square_out_ref.shape)
    square_copy = pltpu.make_async_remote_copy(
        src_ref=square_out_ref,
        dst_ref=square_in_ref,
        send_sem=square_send,
        recv_sem=square_recv,
        device_id={"tensor": peer},
        device_id_type=MESH,
    )
    square_copy.start()
    weight_load.wait()
    own_width = out_ref.shape[1]
    tile_count = own_width // TILE

    def tile_copy(tile):
        return pltpu.make_async_remote_copy(
            src_ref=sent_ref.at[tile],
            dst_ref=landed_ref.at[tile],
            send_sem=tile_send.at[tile],
            recv_sem=tile_recv.at[tile],
            device_id={"tensor": peer},
            device_id_type=MESH,
        )

    def project(owner, tile):
        start = pl.multiple_of(owner * own_width + tile * TILE, LANES)
        return jnp.dot(
            normed_ref[...], weight_ref[:, pl.ds(start, TILE)], preferred_element_type=jnp.float32
        )

    @pl.loop(0, tile_count)
    def _(tile):
        sent_ref[tile] = project(peer, tile).astype(jnp.bfloat16)
        tile_copy(tile).start()

    square_copy.wait()
    inner = 2 * heads * HEAD_DIM
    scale = lax.rsqrt((square_out_ref[0:1, :] + square_in_ref[0:1, :]) / inner + EPSILON)
    square_ref[...] = jnp.broadcast_to(scale, (LANES, STRETCH)).T

    @pl.loop(0, tile_count)
    def _(tile):
        own = project(tensor_index, tile)
        tile_copy(tile).wait_recv()
        both = own + landed_ref[tile].astype(jnp.float32)
        scales = square_ref[...]
        for side in range(TILE // LANES):
            start = pl.multiple_of(tile * TILE + side * LANES, LANES)
            out_ref[:, pl.ds(start, LANES)] = (
                both[:, side * LANES : (side + 1) * LANES] * scales
            ).astype(jnp.bfloat16)

    @pl.loop(0, tile_count)
    def _(tile):
        tile_copy(tile).wait_send()

    @pl.when(place < places - 1)
    def _():
        @pl.loop(0, chunk_count)
        def _(chunk):
            chain_copy(chunk).wait_send()


def fused_on_device(
    span_count,
    band_count,
    signal,
    gate_branch,
    write_proj,
    read_proj,
    step_logits,
    valid_mask,
    stretch_band,
    band_offset,
    decay_log,
    step_offset,
    skip_gain,
    norm_gain,
    out_weight,
):
    heads = decay_log.shape[0]
    inner = heads * HEAD_DIM
    width = out_weight.shape[1]
    pair_count = heads // 2
    chunk_count = pair_count // PAIRS
    tile_count = width // 2 // TILE
    vmem = pl.BlockSpec(memory_space=pltpu.VMEM)
    hbm = pl.BlockSpec(memory_space=pl.ANY)
    smem = pl.BlockSpec(memory_space=pltpu.SMEM)
    f32, bf16 = jnp.float32, jnp.bfloat16
    return pl.pallas_call(
        functools.partial(fused_kernel, heads, span_count, band_count),
        out_shape=jax.ShapeDtypeStruct((STRETCH, width // 2), bf16),
        in_specs=[vmem, hbm] + [vmem] * 4 + [smem] + [vmem] * 5 + [hbm],
        out_specs=vmem,
        scratch_shapes=[
            pltpu.VMEM((inner, width), bf16),
            pltpu.VMEM((STRETCH, inner), bf16),
            pltpu.VMEM((LANES, STRETCH), f32),
            pltpu.VMEM((8, LANES), f32),
            pltpu.VMEM((LANES, STRETCH), f32),
            pltpu.VMEM((STRETCH, 2 * LANES), bf16),
            pltpu.VMEM((16, LANES), bf16),
            pltpu.VMEM((STRETCH, STRETCH), f32),
            pltpu.VMEM((STATE, STRETCH), bf16),
            pltpu.VMEM((pair_count, STRETCH, 2 * LANES), f32),
            pltpu.VMEM((STRETCH, inner), f32),
            pltpu.VMEM((STRETCH, inner), bf16),
            pltpu.VMEM((pair_count, STATE, LANES), f32),
            pltpu.VMEM((pair_count, 8, LANES), f32),
            pltpu.VMEM((STRETCH, inner), f32),
            pltpu.VMEM((STRETCH, inner), bf16),
            pltpu.VMEM((STRETCH, LANES), f32),
            pltpu.VMEM((chunk_count, PAIRS, STATE, LANES), bf16),
            pltpu.VMEM((chunk_count, PAIRS, STATE, LANES), bf16),
            pltpu.VMEM((tile_count, STRETCH, TILE), bf16),
            pltpu.VMEM((tile_count, STRETCH, TILE), bf16),
            pltpu.VMEM((8, STRETCH), f32),
            pltpu.VMEM((8, STRETCH), f32),
            pltpu.SemaphoreType.DMA((2,)),
            pltpu.SemaphoreType.DMA((chunk_count,)),
            pltpu.SemaphoreType.DMA((chunk_count,)),
            pltpu.SemaphoreType.DMA((tile_count,)),
            pltpu.SemaphoreType.DMA((tile_count,)),
            pltpu.SemaphoreType.DMA,
            pltpu.SemaphoreType.DMA,
        ],
        compiler_params=pltpu.CompilerParams(
            collective_id=0, has_side_effects=True, vmem_limit_bytes=60 * 1024 * 1024
        ),
    )(
        signal,
        gate_branch,
        write_proj,
        read_proj,
        step_logits,
        valid_mask[None, :],
        stretch_band,
        band_offset,
        decay_log[None, :],
        step_offset[None, :],
        skip_gain[None, :],
        norm_gain[None, :],
        out_weight,
    )


def solution(mesh):
    placed = (
        P(("group", "scan", "band"), "tensor"),
        P(("group", "scan", "band"), "tensor"),
        P(("group", "scan", "band"), None),
        P(("group", "scan", "band"), None),
        P("tensor", ("group", "scan", "band")),
        P(("group", "scan", "band")),
        P(("group", "scan", "band")),
        P(None, "tensor"),
        P("tensor"),
        P("tensor"),
        P("tensor"),
        P("tensor"),
        P("tensor", None),
    )
    shape = dict(mesh.shape)
    places = shape["scan"] * shape["band"]

    def layer(*arrays):
        rows = arrays[0].shape[0] // (shape["group"] * places)
        heads = arrays[8].shape[0] // shape["tensor"]
        width = arrays[12].shape[1]
        fits = (
            shape["tensor"] == 2
            and places > 2
            and rows == STRETCH
            and heads % (2 * PAIRS) == 0
            and 3 * heads <= LANES
            and width % (2 * TILE) == 0
        )
        member = on_device
        if fits:
            member = functools.partial(fused_on_device, shape["scan"], shape["band"])
        return mapped(member)(*arrays)

    def mapped(member):
        return jax.shard_map(
            member,
            mesh=mesh,
            in_specs=placed,
            out_specs=P(("group", "scan", "band"), "tensor"),
            check_vma=False,
        )

    return layer
```

```python
import functools

import jax
import jax.numpy as jnp
from jax import lax
from jax.experimental import pallas as pl
from jax.experimental.pallas import tpu as pltpu
from jax.sharding import PartitionSpec as P

HEAD_DIM = 64
STATE = 128
STRETCH = 256
BANDS = 12
INNER = 5120


EPSILON = 1e-05
HIGHEST = lax.Precision.HIGHEST


def step_sizes(step_logits, stretch_band, band_offset, step_offset):
    one_hot = (stretch_band[:, None] == jnp.arange(BANDS, dtype=jnp.int32)[None, :]).astype(
        jnp.float32
    )
    stretch_offset = jnp.dot(one_hot, band_offset, precision=HIGHEST)
    token_offset = jnp.repeat(stretch_offset, STRETCH, axis=0).T
    return jax.nn.softplus(step_logits + step_offset[:, None] + token_offset)


def combine(earlier, later_pair):
    return (
        earlier[0] + later_pair[0],
        jnp.exp(later_pair[0])[:, None, None] * earlier[1] + later_pair[1],
    )


def local_step(running_pair, member):
    return (combine(running_pair, member), running_pair)


def on_device(
    signal,
    gate_branch,
    write_proj,
    read_proj,
    step_logits,
    valid_mask,
    stretch_band,
    band_offset,
    decay_log,
    step_offset,
    skip_gain,
    norm_gain,
    out_weight,
):
    row_count = signal.shape[0]
    head_count = decay_log.shape[0]
    block_count = row_count // STRETCH
    step_size = step_sizes(step_logits, stretch_band, band_offset, step_offset)
    log_decay = step_size * (-jnp.exp(decay_log))[:, None]
    input_weight = step_size * valid_mask.astype(jnp.float32)[None, :]
    running = jnp.cumsum(log_decay.reshape(head_count, block_count, STRETCH), axis=2)
    weight_blocks = input_weight.reshape(head_count, block_count, STRETCH)
    signal_blocks = signal.reshape(block_count, STRETCH, head_count, HEAD_DIM)
    write_blocks = write_proj.reshape(block_count, STRETCH, STATE)
    read_blocks = read_proj.reshape(block_count, STRETCH, STATE)
    scores = jnp.einsum(
        "cin,cjn->cij", read_blocks, write_blocks, preferred_element_type=jnp.float32
    )
    lower_mask = jnp.arange(STRETCH)[:, None] >= jnp.arange(STRETCH)[None, :]
    span_logs = jnp.where(
        lower_mask[None, None], running[:, :, :, None] - running[:, :, None, :], -1e30
    )
    mixing = (jnp.exp(span_logs) * scores[None] * weight_blocks[:, :, None, :]).astype(jnp.bfloat16)
    local_out = jnp.einsum(
        "hcij,cjhp->cihp", mixing, signal_blocks, preferred_element_type=jnp.float32
    )
    tail_weight = jnp.exp(running[:, :, -1:] - running) * weight_blocks
    scaled = (
        signal_blocks.astype(jnp.float32) * jnp.transpose(tail_weight, (1, 2, 0))[:, :, :, None]
    ).astype(jnp.bfloat16)
    block_states = jnp.einsum(
        "cjhp,cjn->chpn", scaled, write_blocks, preferred_element_type=jnp.float32
    )
    block_decay = running[:, :, -1].T
    zero_state = jnp.zeros((head_count, HEAD_DIM, STATE), jnp.float32)
    zero_log = jnp.zeros((head_count,), jnp.float32)
    identity = (zero_log, zero_state)
    device_pair, segment_cumulative = lax.scan(local_step, identity, (block_decay, block_states))
    all_logs = lax.all_gather(device_pair[0][None], ("scan", "band"), axis=0, tiled=True)
    inclusive = jnp.cumsum(all_logs, axis=0)
    exclusive = inclusive - all_logs
    position = lax.axis_index(("scan", "band"))
    own_exclusive = lax.dynamic_index_in_dim(exclusive, position, 0, keepdims=False)
    shard_block = lax.all_gather(
        device_pair[1][None].astype(jnp.bfloat16), ("scan", "band"), axis=0, tiled=True
    ).astype(jnp.float32)
    how_many = shard_block.shape[0]
    sources = jnp.arange(how_many, dtype=jnp.int32)
    gap_logs = jnp.where((sources < position)[:, None], own_exclusive[None, :] - inclusive, -1e30)
    carry_state = zero_state + jnp.einsum(
        "kh,khpn->hpn", jnp.exp(gap_logs), shard_block, precision=HIGHEST
    )
    enter_state = (
        jnp.exp(segment_cumulative[0])[:, :, None, None] * carry_state[None] + segment_cumulative[1]
    )
    state_high = enter_state.astype(jnp.bfloat16)
    widened = lax.optimization_barrier(state_high).astype(jnp.float32)
    state_low = (enter_state - widened).astype(jnp.bfloat16)
    high_part = jnp.einsum(
        "cin,chpn->cihp", read_blocks, state_high, preferred_element_type=jnp.float32
    )
    low_part = jnp.einsum(
        "cin,chpn->cihp", read_blocks, state_low, preferred_element_type=jnp.float32
    )
    carried_out = jnp.transpose(jnp.exp(running), (1, 2, 0))[:, :, :, None] * (high_part + low_part)
    ssm_out = (local_out + carried_out).reshape(row_count, head_count, HEAD_DIM) + skip_gain[
        None, :, None
    ] * signal.reshape(row_count, head_count, HEAD_DIM).astype(jnp.float32)
    gated_out = ssm_out.reshape(row_count, head_count * HEAD_DIM) * jax.nn.silu(
        gate_branch.astype(jnp.float32)
    )
    square_total = lax.psum(jnp.sum(gated_out * gated_out, axis=1), "tensor")
    normed = (
        gated_out * lax.rsqrt(square_total / INNER + EPSILON)[:, None] * norm_gain[None, :]
    ).astype(jnp.bfloat16)
    own_columns = lax.psum_scatter(
        lax.dot_general(
            out_weight, normed, (((0,), (1,)), ((), ())), preferred_element_type=jnp.float32
        ).astype(jnp.bfloat16),
        "tensor",
        scatter_dimension=0,
        tiled=True,
    ).astype(jnp.float32)
    return own_columns.T.astype(jnp.bfloat16)


LOG2E = 1.4426950408889634
LANES = 128
PAIRS = 1
GROUP = 4
TILE = 256
MESH = pl.DeviceIdType.MESH


def fused_kernel(
    heads,
    span_count,
    band_count,
    signal_ref,
    gate_hbm,
    write_ref,
    read_ref,
    logits_ref,
    valid_ref,
    band_ref,
    offset_ref,
    decay_ref,
    bias_ref,
    skip_ref,
    gain_ref,
    weight_hbm,
    out_ref,
    weight_ref,
    gate_ref,
    padded_ref,
    params_ref,
    row_ref,
    spread_ref,
    skip_rows_ref,
    scores_ref,
    read_by_token_ref,
    lead_ref,
    fed_ref,
    state_ref,
    total_ref,
    local_ref,
    normed_ref,
    square_ref,
    carry_ref,
    pass_ref,
    sent_ref,
    landed_ref,
    square_out_ref,
    square_in_ref,
    load_sem,
    chain_send,
    chain_recv,
    tile_send,
    tile_recv,
    square_send,
    square_recv,
):
    pair_count = heads // 2
    chunk_count = pair_count // PAIRS
    places = span_count * band_count
    scan_index = lax.axis_index("scan")
    band_index = lax.axis_index("band")
    tensor_index = lax.axis_index("tensor")
    place = scan_index * band_count + band_index
    following = lax.rem(place + 1, places)
    previous = lax.rem(place + places - 1, places)
    peer = 1 - tensor_index

    def at_place(spot):
        return {"scan": spot // band_count, "band": lax.rem(spot, band_count)}

    barrier = pltpu.get_barrier_semaphore()
    for target in (at_place(following), at_place(previous), {"tensor": peer}):
        pl.semaphore_signal(barrier, inc=1, device_id=target, device_id_type=MESH)
    gate_load = pltpu.make_async_copy(gate_hbm, gate_ref, load_sem.at[0])
    weight_load = pltpu.make_async_copy(weight_hbm, weight_ref, load_sem.at[1])
    gate_load.start()
    weight_load.start()

    padded_ref[...] = jnp.zeros_like(padded_ref)
    padded_ref[0:heads, :] = logits_ref[...]
    params_ref[...] = jnp.zeros_like(params_ref)
    chosen = lax.broadcasted_iota(jnp.int32, (BANDS, heads), 0) == band_ref[0]
    params_ref[0:1, 0:heads] = bias_ref[...] + jnp.sum(
        jnp.where(chosen, offset_ref[...], 0.0), axis=0, keepdims=True
    )
    params_ref[1:2, 0:heads] = jnp.exp(decay_ref[...])
    params_ref[2:3, 0:heads] = skip_ref[...]
    shifted = padded_ref[...].T + params_ref[0:1, :]
    step_size = jnp.maximum(shifted, 0.0) + jnp.log1p(jnp.exp(-jnp.abs(shifted)))
    lanes = lax.broadcasted_iota(jnp.int32, (STRETCH, LANES), 1)
    tokens = lax.broadcasted_iota(jnp.int32, (STRETCH, LANES), 0)
    real = lanes < heads
    running = jnp.where(real, step_size * -params_ref[1:2, :], 0.0)
    shift = 1
    while shift < STRETCH:
        running = running + jnp.where(tokens >= shift, pltpu.roll(running, shift, 0), 0.0)
        shift *= 2
    running = running * LOG2E
    row_ref[...] = running.T
    valid = jnp.broadcast_to(valid_ref[...].astype(jnp.float32), (LANES, STRETCH)).T
    in_weight = jnp.where(real, step_size * valid, 0.0)

    def three_parts(value):
        high = value.astype(jnp.bfloat16).astype(jnp.float32)
        rest = value - high
        middle = rest.astype(jnp.bfloat16).astype(jnp.float32)
        low = rest - middle
        packed = high + pltpu.roll(middle, heads, 1) + pltpu.roll(low, 2 * heads, 1)
        return packed.astype(jnp.bfloat16)

    spread_ref[:, 0:LANES] = three_parts(running)
    spread_ref[:, LANES : 2 * LANES] = three_parts(in_weight)
    skip_rows_ref[...] = three_parts(jnp.broadcast_to(params_ref[2:3, :], (16, LANES)))
    write_turned = write_ref[...].astype(jnp.float32).T.astype(jnp.bfloat16)
    read_by_token_ref[...] = write_turned
    scores = jnp.dot(read_ref[...], write_turned, preferred_element_type=jnp.float32)
    square_rows = lax.broadcasted_iota(jnp.int32, (STRETCH, STRETCH), 0)
    square_columns = lax.broadcasted_iota(jnp.int32, (STRETCH, STRETCH), 1)
    scores_ref[...] = jnp.where(square_columns <= square_rows, scores, 0.0)
    square_ref[...] = jnp.zeros_like(square_ref)

    @pl.when(place == 0)
    def _():
        carry_ref[...] = jnp.zeros_like(carry_ref)

    pl.semaphore_wait(barrier, 3)

    def chain_copy(chunk):
        return pltpu.make_async_remote_copy(
            src_ref=pass_ref.at[chunk],
            dst_ref=carry_ref.at[chunk],
            send_sem=chain_send.at[chunk],
            recv_sem=chain_recv.at[chunk],
            device_id=at_place(following),
            device_id_type=MESH,
        )

    def chain_step(chunk):
        @pl.when(place > 0)
        def _():
            chain_copy(chunk).wait_recv()

        @pl.when(place < places - 1)
        def _():
            for member in range(PAIRS):
                pair = chunk * PAIRS + member
                onward = (
                    total_ref[pair][0:1, :] * carry_ref[chunk, member].astype(jnp.float32)
                    + state_ref[pair]
                )
                pass_ref[chunk, member] = onward.astype(jnp.bfloat16)
            chain_copy(chunk).start()

    def columns_of(pair):
        return pl.ds(pl.multiple_of(pair * LANES, LANES), LANES)

    part = lax.broadcasted_iota(jnp.int32, (LANES, 2 * LANES), 0)
    part = (
        part
        - jnp.where(part >= heads, heads, 0)
        - jnp.where(part >= 2 * heads, heads, 0)
    )
    wide_side = lax.broadcasted_iota(jnp.int32, (LANES, 2 * LANES), 1) // LANES
    wide_index = part - wide_side
    narrow_side = lax.broadcasted_iota(jnp.int32, (LANES, LANES), 1) // HEAD_DIM
    narrow_index = part[:, 0:LANES] - narrow_side
    outside = jnp.full((LANES, LANES), -1, jnp.int32)
    block_index = jnp.concatenate(
        [
            jnp.concatenate([narrow_index, outside], axis=1),
            jnp.concatenate([outside, narrow_index], axis=1),
        ],
        axis=0,
    )
    first_half = lanes < HEAD_DIM

    def picker(index, pair):
        return jnp.where(index == 2 * pair, 1.0, 0.0).astype(jnp.bfloat16)

    def state_pair(pair):
        columns = columns_of(pair)
        both = jnp.dot(
            spread_ref[...], picker(block_index, pair), preferred_element_type=jnp.float32
        )
        own_run = both[:, 0:LANES]
        weight = both[:, LANES : 2 * LANES]
        last_run = own_run[STRETCH - 1 : STRETCH, :]
        fed = signal_ref[:, columns].astype(jnp.float32) * weight
        fed_ref[:, columns] = fed.astype(jnp.bfloat16)
        lead_ref[:, columns] = jnp.exp2(own_run)
        scaled = (fed * jnp.exp2(last_run - own_run)).astype(jnp.bfloat16)
        state_ref[pair] = jnp.dot(
            read_by_token_ref[...], scaled, preferred_element_type=jnp.float32
        )
        total_ref[pair] = jnp.broadcast_to(jnp.exp2(last_run), (8, LANES))

    def mix_pair(pair):
        columns = columns_of(pair)
        half = STRETCH // 2
        tops, bottoms = [], []
        fed = fed_ref[:, columns]
        runs = jnp.dot(
            spread_ref[:, 0:LANES], picker(wide_index, pair), preferred_element_type=jnp.float32
        )
        for side in range(2):
            row = row_ref[pl.ds(2 * pair + side, 1), :]
            run = runs[:, side * LANES : (side + 1) * LANES]
            near = jnp.exp2(jnp.minimum(run[0:half] - row[:, 0:half], 0.0))
            far = jnp.exp2(jnp.minimum(run[half:] - row[:, 0:half], 0.0))
            late = jnp.exp2(jnp.minimum(run[half:] - row[:, half:], 0.0))
            near = (near * scores_ref[0:half, 0:half]).astype(jnp.bfloat16)
            far = (far * scores_ref[half:, 0:half]).astype(jnp.bfloat16)
            late = (late * scores_ref[half:, half:]).astype(jnp.bfloat16)
            tops.append(jnp.dot(near, fed[0:half], preferred_element_type=jnp.float32))
            bottoms.append(
                jnp.dot(
                    jnp.concatenate([far, late], axis=1), fed, preferred_element_type=jnp.float32
                )
            )
        local_ref[0:half, columns] = jnp.where(first_half[0:half], tops[0], tops[1])
        local_ref[half:, columns] = jnp.where(first_half[half:], bottoms[0], bottoms[1])

    def gate_pair(chunk, member):
        pair = chunk * PAIRS + member
        columns = columns_of(pair)
        carried = jnp.dot(
            read_ref[...], carry_ref[chunk, member], preferred_element_type=jnp.float32
        )
        skip = jnp.dot(
            skip_rows_ref[...], picker(narrow_index, pair), preferred_element_type=jnp.float32
        )
        ssm_out = (
            local_ref[:, columns]
            + lead_ref[:, columns] * carried
            + skip[0:1, :] * signal_ref[:, columns].astype(jnp.float32)
        )
        gate = gate_ref[:, columns].astype(jnp.float32)
        gated = ssm_out * (gate / (1.0 + jnp.exp(-gate)))
        square_ref[...] += gated * gated
        normed_ref[:, columns] = (gated * gain_ref[pl.ds(pair, 1), :]).astype(jnp.bfloat16)

    @pl.loop(0, chunk_count // GROUP)
    def _(group):
        for member in range(GROUP * PAIRS):
            state_pair(group * GROUP * PAIRS + member)

        @pl.when(place == 0)
        def _():
            for member in range(GROUP):
                chain_step(group * GROUP + member)

    delay = jnp.minimum(chunk_count, place * 6)

    def chain_slot(slot):
        chunk = slot - delay

        @pl.when((place > 0) & (chunk >= 0) & (chunk < chunk_count))
        def _():
            chain_step(chunk)

    @pl.loop(0, chunk_count)
    def _(slot):
        chain_slot(slot)
        for member in range(PAIRS):
            mix_pair(slot * PAIRS + member)

    gate_load.wait()

    @pl.loop(0, chunk_count)
    def _(slot):
        chain_slot(slot + chunk_count)
        for member in range(PAIRS):
            gate_pair(slot, member)

    square_sum = jnp.sum(square_ref[...].T, axis=0, keepdims=True)
    square_out_ref[...] = jnp.broadcast_to(square_sum, square_out_ref.shape)
    square_copy = pltpu.make_async_remote_copy(
        src_ref=square_out_ref,
        dst_ref=square_in_ref,
        send_sem=square_send,
        recv_sem=square_recv,
        device_id={"tensor": peer},
        device_id_type=MESH,
    )
    square_copy.start()
    weight_load.wait()
    own_width = out_ref.shape[1]
    tile_count = own_width // TILE

    def tile_copy(tile):
        return pltpu.make_async_remote_copy(
            src_ref=sent_ref.at[tile],
            dst_ref=landed_ref.at[tile],
            send_sem=tile_send.at[tile],
            recv_sem=tile_recv.at[tile],
            device_id={"tensor": peer},
            device_id_type=MESH,
        )

    def project(owner, tile):
        start = pl.multiple_of(owner * own_width + tile * TILE, LANES)
        return jnp.dot(
            normed_ref[...], weight_ref[:, pl.ds(start, TILE)], preferred_element_type=jnp.float32
        )

    @pl.loop(0, tile_count)
    def _(tile):
        sent_ref[tile] = project(peer, tile).astype(jnp.bfloat16)
        tile_copy(tile).start()

    square_copy.wait()
    inner = 2 * heads * HEAD_DIM
    scale = lax.rsqrt((square_out_ref[0:1, :] + square_in_ref[0:1, :]) / inner + EPSILON)
    square_ref[...] = jnp.broadcast_to(scale, (LANES, STRETCH)).T

    @pl.loop(0, tile_count)
    def _(tile):
        own = project(tensor_index, tile)
        tile_copy(tile).wait_recv()
        both = own + landed_ref[tile].astype(jnp.float32)
        scales = square_ref[...]
        for side in range(TILE // LANES):
            start = pl.multiple_of(tile * TILE + side * LANES, LANES)
            out_ref[:, pl.ds(start, LANES)] = (
                both[:, side * LANES : (side + 1) * LANES] * scales
            ).astype(jnp.bfloat16)

    @pl.loop(0, tile_count)
    def _(tile):
        tile_copy(tile).wait_send()

    @pl.when(place < places - 1)
    def _():
        @pl.loop(0, chunk_count)
        def _(chunk):
            chain_copy(chunk).wait_send()


def fused_on_device(
    span_count,
    band_count,
    signal,
    gate_branch,
    write_proj,
    read_proj,
    step_logits,
    valid_mask,
    stretch_band,
    band_offset,
    decay_log,
    step_offset,
    skip_gain,
    norm_gain,
    out_weight,
):
    heads = decay_log.shape[0]
    inner = heads * HEAD_DIM
    width = out_weight.shape[1]
    pair_count = heads // 2
    chunk_count = pair_count // PAIRS
    tile_count = width // 2 // TILE
    vmem = pl.BlockSpec(memory_space=pltpu.VMEM)
    hbm = pl.BlockSpec(memory_space=pl.ANY)
    smem = pl.BlockSpec(memory_space=pltpu.SMEM)
    f32, bf16 = jnp.float32, jnp.bfloat16
    return pl.pallas_call(
        functools.partial(fused_kernel, heads, span_count, band_count),
        out_shape=pltpu.VMEM((STRETCH, width // 2), bf16),
        in_specs=[vmem, hbm] + [vmem] * 4 + [smem] + [vmem] * 5 + [hbm],
        out_specs=vmem,
        scratch_shapes=[
            pltpu.VMEM((inner, width), bf16),
            pltpu.VMEM((STRETCH, inner), bf16),
            pltpu.VMEM((LANES, STRETCH), f32),
            pltpu.VMEM((8, LANES), f32),
            pltpu.VMEM((LANES, STRETCH), f32),
            pltpu.VMEM((STRETCH, 2 * LANES), bf16),
            pltpu.VMEM((16, LANES), bf16),
            pltpu.VMEM((STRETCH, STRETCH), f32),
            pltpu.VMEM((STATE, STRETCH), bf16),
            pltpu.VMEM((STRETCH, inner), f32),
            pltpu.VMEM((STRETCH, inner), bf16),
            pltpu.VMEM((pair_count, STATE, LANES), f32),
            pltpu.VMEM((pair_count, 8, LANES), f32),
            pltpu.VMEM((STRETCH, inner), f32),
            pltpu.VMEM((STRETCH, inner), bf16),
            pltpu.VMEM((STRETCH, LANES), f32),
            pltpu.VMEM((chunk_count, PAIRS, STATE, LANES), bf16),
            pltpu.VMEM((chunk_count, PAIRS, STATE, LANES), bf16),
            pltpu.VMEM((tile_count, STRETCH, TILE), bf16),
            pltpu.VMEM((tile_count, STRETCH, TILE), bf16),
            pltpu.VMEM((8, STRETCH), f32),
            pltpu.VMEM((8, STRETCH), f32),
            pltpu.SemaphoreType.DMA((2,)),
            pltpu.SemaphoreType.DMA((chunk_count,)),
            pltpu.SemaphoreType.DMA((chunk_count,)),
            pltpu.SemaphoreType.DMA((tile_count,)),
            pltpu.SemaphoreType.DMA((tile_count,)),
            pltpu.SemaphoreType.DMA,
            pltpu.SemaphoreType.DMA,
        ],
        compiler_params=pltpu.CompilerParams(
            collective_id=0, has_side_effects=True, vmem_limit_bytes=60 * 1024 * 1024
        ),
    )(
        signal,
        gate_branch,
        write_proj,
        read_proj,
        step_logits,
        valid_mask[None, :],
        stretch_band,
        band_offset,
        decay_log[None, :],
        step_offset[None, :],
        skip_gain[None, :],
        norm_gain.reshape(pair_count, LANES),
        out_weight,
    )


def solution(mesh):
    placed = (
        P(("group", "scan", "band"), "tensor"),
        P(("group", "scan", "band"), "tensor"),
        P(("group", "scan", "band"), None),
        P(("group", "scan", "band"), None),
        P("tensor", ("group", "scan", "band")),
        P(("group", "scan", "band")),
        P(("group", "scan", "band")),
        P(None, "tensor"),
        P("tensor"),
        P("tensor"),
        P("tensor"),
        P("tensor"),
        P("tensor", None),
    )
    shape = dict(mesh.shape)
    places = shape["scan"] * shape["band"]

    def layer(*arrays):
        rows = arrays[0].shape[0] // (shape["group"] * places)
        heads = arrays[8].shape[0] // shape["tensor"]
        width = arrays[12].shape[1]
        fits = (
            shape["tensor"] == 2
            and places > 2
            and rows == STRETCH
            and heads % (2 * PAIRS * GROUP) == 0
            and 3 * heads <= LANES
            and width % (2 * TILE) == 0
        )
        member = on_device
        if fits:
            member = functools.partial(fused_on_device, shape["scan"], shape["band"])
        return mapped(member)(*arrays)

    def mapped(member):
        return jax.shard_map(
            member,
            mesh=mesh,
            in_specs=placed,
            out_specs=P(("group", "scan", "band"), "tensor"),
            check_vma=False,
        )

    return layer
```

```python
import functools

import jax
import jax.numpy as jnp
from jax import lax
from jax.experimental import pallas as pl
from jax.experimental.pallas import tpu as pltpu
from jax.sharding import PartitionSpec as P

HEAD_DIM = 64
STATE = 128
STRETCH = 256
BANDS = 12
INNER = 5120


EPSILON = 1e-05
HIGHEST = lax.Precision.HIGHEST


def step_sizes(step_logits, stretch_band, band_offset, step_offset):
    one_hot = (stretch_band[:, None] == jnp.arange(BANDS, dtype=jnp.int32)[None, :]).astype(
        jnp.float32
    )
    stretch_offset = jnp.dot(one_hot, band_offset, precision=HIGHEST)
    token_offset = jnp.repeat(stretch_offset, STRETCH, axis=0).T
    return jax.nn.softplus(step_logits + step_offset[:, None] + token_offset)


def combine(earlier, later_pair):
    return (
        earlier[0] + later_pair[0],
        jnp.exp(later_pair[0])[:, None, None] * earlier[1] + later_pair[1],
    )


def local_step(running_pair, member):
    return (combine(running_pair, member), running_pair)


def on_device(
    signal,
    gate_branch,
    write_proj,
    read_proj,
    step_logits,
    valid_mask,
    stretch_band,
    band_offset,
    decay_log,
    step_offset,
    skip_gain,
    norm_gain,
    out_weight,
):
    row_count = signal.shape[0]
    head_count = decay_log.shape[0]
    block_count = row_count // STRETCH
    step_size = step_sizes(step_logits, stretch_band, band_offset, step_offset)
    log_decay = step_size * (-jnp.exp(decay_log))[:, None]
    input_weight = step_size * valid_mask.astype(jnp.float32)[None, :]
    running = jnp.cumsum(log_decay.reshape(head_count, block_count, STRETCH), axis=2)
    weight_blocks = input_weight.reshape(head_count, block_count, STRETCH)
    signal_blocks = signal.reshape(block_count, STRETCH, head_count, HEAD_DIM)
    write_blocks = write_proj.reshape(block_count, STRETCH, STATE)
    read_blocks = read_proj.reshape(block_count, STRETCH, STATE)
    scores = jnp.einsum(
        "cin,cjn->cij", read_blocks, write_blocks, preferred_element_type=jnp.float32
    )
    lower_mask = jnp.arange(STRETCH)[:, None] >= jnp.arange(STRETCH)[None, :]
    span_logs = jnp.where(
        lower_mask[None, None], running[:, :, :, None] - running[:, :, None, :], -1e30
    )
    mixing = (jnp.exp(span_logs) * scores[None] * weight_blocks[:, :, None, :]).astype(jnp.bfloat16)
    local_out = jnp.einsum(
        "hcij,cjhp->cihp", mixing, signal_blocks, preferred_element_type=jnp.float32
    )
    tail_weight = jnp.exp(running[:, :, -1:] - running) * weight_blocks
    scaled = (
        signal_blocks.astype(jnp.float32) * jnp.transpose(tail_weight, (1, 2, 0))[:, :, :, None]
    ).astype(jnp.bfloat16)
    block_states = jnp.einsum(
        "cjhp,cjn->chpn", scaled, write_blocks, preferred_element_type=jnp.float32
    )
    block_decay = running[:, :, -1].T
    zero_state = jnp.zeros((head_count, HEAD_DIM, STATE), jnp.float32)
    zero_log = jnp.zeros((head_count,), jnp.float32)
    identity = (zero_log, zero_state)
    device_pair, segment_cumulative = lax.scan(local_step, identity, (block_decay, block_states))
    all_logs = lax.all_gather(device_pair[0][None], ("scan", "band"), axis=0, tiled=True)
    inclusive = jnp.cumsum(all_logs, axis=0)
    exclusive = inclusive - all_logs
    position = lax.axis_index(("scan", "band"))
    own_exclusive = lax.dynamic_index_in_dim(exclusive, position, 0, keepdims=False)
    shard_block = lax.all_gather(
        device_pair[1][None].astype(jnp.bfloat16), ("scan", "band"), axis=0, tiled=True
    ).astype(jnp.float32)
    how_many = shard_block.shape[0]
    sources = jnp.arange(how_many, dtype=jnp.int32)
    gap_logs = jnp.where((sources < position)[:, None], own_exclusive[None, :] - inclusive, -1e30)
    carry_state = zero_state + jnp.einsum(
        "kh,khpn->hpn", jnp.exp(gap_logs), shard_block, precision=HIGHEST
    )
    enter_state = (
        jnp.exp(segment_cumulative[0])[:, :, None, None] * carry_state[None] + segment_cumulative[1]
    )
    state_high = enter_state.astype(jnp.bfloat16)
    widened = lax.optimization_barrier(state_high).astype(jnp.float32)
    state_low = (enter_state - widened).astype(jnp.bfloat16)
    high_part = jnp.einsum(
        "cin,chpn->cihp", read_blocks, state_high, preferred_element_type=jnp.float32
    )
    low_part = jnp.einsum(
        "cin,chpn->cihp", read_blocks, state_low, preferred_element_type=jnp.float32
    )
    carried_out = jnp.transpose(jnp.exp(running), (1, 2, 0))[:, :, :, None] * (high_part + low_part)
    ssm_out = (local_out + carried_out).reshape(row_count, head_count, HEAD_DIM) + skip_gain[
        None, :, None
    ] * signal.reshape(row_count, head_count, HEAD_DIM).astype(jnp.float32)
    gated_out = ssm_out.reshape(row_count, head_count * HEAD_DIM) * jax.nn.silu(
        gate_branch.astype(jnp.float32)
    )
    square_total = lax.psum(jnp.sum(gated_out * gated_out, axis=1), "tensor")
    normed = (
        gated_out * lax.rsqrt(square_total / INNER + EPSILON)[:, None] * norm_gain[None, :]
    ).astype(jnp.bfloat16)
    own_columns = lax.psum_scatter(
        lax.dot_general(
            out_weight, normed, (((0,), (1,)), ((), ())), preferred_element_type=jnp.float32
        ).astype(jnp.bfloat16),
        "tensor",
        scatter_dimension=0,
        tiled=True,
    ).astype(jnp.float32)
    return own_columns.T.astype(jnp.bfloat16)


LOG2E = 1.4426950408889634
LANES = 128
PAIRS = 2
STATE_PAIRS = 4
MIX_PAIRS = 4
GATE_PAIRS = 2
SLOTS = 2
TILE = 256
MESH = pl.DeviceIdType.MESH


def fused_kernel(
    heads,
    span_count,
    band_count,
    signal_hbm,
    gate_hbm,
    write_ref,
    read_ref,
    logits_ref,
    valid_ref,
    band_ref,
    offset_ref,
    decay_ref,
    bias_ref,
    skip_ref,
    gain_ref,
    weight_hbm,
    out_ref,
    weight_ref,
    signal_ref,
    gate_ref,
    padded_ref,
    params_ref,
    row_ref,
    spread_ref,
    skip_rows_ref,
    scores_ref,
    read_by_token_ref,
    lead_ref,
    fed_ref,
    state_ref,
    total_ref,
    local_ref,
    normed_ref,
    square_ref,
    carry_ref,
    pass_ref,
    sent_ref,
    landed_ref,
    square_out_ref,
    square_in_ref,
    load_sem,
    chain_send,
    chain_recv,
    tile_send,
    tile_recv,
    square_send,
    square_recv,
):
    pair_count = heads // 2
    chunk_count = pair_count // PAIRS
    places = span_count * band_count
    scan_index = lax.axis_index("scan")
    band_index = lax.axis_index("band")
    tensor_index = lax.axis_index("tensor")
    place = scan_index * band_count + band_index
    following = lax.rem(place + 1, places)
    previous = lax.rem(place + places - 1, places)
    peer = 1 - tensor_index

    def at_place(spot):
        return {"scan": spot // band_count, "band": lax.rem(spot, band_count)}

    barrier = pltpu.get_barrier_semaphore()
    for target in (at_place(following), at_place(previous), {"tensor": peer}):
        pl.semaphore_signal(barrier, inc=1, device_id=target, device_id_type=MESH)
    signal_load = pltpu.make_async_copy(signal_hbm, signal_ref, load_sem.at[2])
    gate_load = pltpu.make_async_copy(gate_hbm, gate_ref, load_sem.at[0])
    weight_load = pltpu.make_async_copy(weight_hbm, weight_ref, load_sem.at[1])
    signal_load.start()
    gate_load.start()
    weight_load.start()

    padded_ref[...] = jnp.zeros_like(padded_ref)
    padded_ref[0:heads, :] = logits_ref[...]
    params_ref[...] = jnp.zeros_like(params_ref)
    chosen = lax.broadcasted_iota(jnp.int32, (BANDS, heads), 0) == band_ref[0]
    params_ref[0:1, 0:heads] = bias_ref[...] + jnp.sum(
        jnp.where(chosen, offset_ref[...], 0.0), axis=0, keepdims=True
    )
    params_ref[1:2, 0:heads] = jnp.exp(decay_ref[...])
    params_ref[2:3, 0:heads] = skip_ref[...]
    shifted = padded_ref[...].T + params_ref[0:1, :]
    step_size = jnp.maximum(shifted, 0.0) + jnp.log1p(jnp.exp(-jnp.abs(shifted)))
    lanes = lax.broadcasted_iota(jnp.int32, (STRETCH, LANES), 1)
    tokens = lax.broadcasted_iota(jnp.int32, (STRETCH, LANES), 0)
    real = lanes < heads
    running = jnp.where(real, step_size * -params_ref[1:2, :], 0.0)
    shift = 1
    while shift < STRETCH:
        running = running + jnp.where(tokens >= shift, pltpu.roll(running, shift, 0), 0.0)
        shift *= 2
    running = running * LOG2E
    row_ref[...] = running.T
    valid = jnp.broadcast_to(valid_ref[...].astype(jnp.float32), (LANES, STRETCH)).T
    in_weight = jnp.where(real, step_size * valid, 0.0)

    def three_parts(value):
        high = value.astype(jnp.bfloat16).astype(jnp.float32)
        rest = value - high
        middle = rest.astype(jnp.bfloat16).astype(jnp.float32)
        low = rest - middle
        packed = high + pltpu.roll(middle, heads, 1) + pltpu.roll(low, 2 * heads, 1)
        return packed.astype(jnp.bfloat16)

    spread_ref[:, 0:LANES] = three_parts(running)
    spread_ref[:, LANES : 2 * LANES] = three_parts(in_weight)
    skip_rows_ref[...] = three_parts(jnp.broadcast_to(params_ref[2:3, :], (16, LANES)))
    write_turned = write_ref[...].astype(jnp.float32).T.astype(jnp.bfloat16)
    read_by_token_ref[...] = write_turned
    scores = jnp.dot(read_ref[...], write_turned, preferred_element_type=jnp.float32)
    square_rows = lax.broadcasted_iota(jnp.int32, (STRETCH, STRETCH), 0)
    square_columns = lax.broadcasted_iota(jnp.int32, (STRETCH, STRETCH), 1)
    scores_ref[...] = jnp.where(square_columns <= square_rows, scores, 0.0)
    square_ref[...] = jnp.zeros_like(square_ref)

    @pl.when(place == 0)
    def _():
        carry_ref[...] = jnp.zeros_like(carry_ref)

    signal_load.wait()
    pl.semaphore_wait(barrier, 3)

    def chain_copy(chunk):
        return pltpu.make_async_remote_copy(
            src_ref=pass_ref.at[chunk],
            dst_ref=carry_ref.at[chunk],
            send_sem=chain_send.at[chunk],
            recv_sem=chain_recv.at[chunk],
            device_id=at_place(following),
            device_id_type=MESH,
        )

    def chain_step(chunk):
        @pl.when(place > 0)
        def _():
            chain_copy(chunk).wait_recv()

        @pl.when(place < places - 1)
        def _():
            for member in range(PAIRS):
                pair = chunk * PAIRS + member
                onward = (
                    total_ref[pair][0:1, :] * carry_ref[chunk, member].astype(jnp.float32)
                    + state_ref[pair]
                )
                pass_ref[chunk, member] = onward.astype(jnp.bfloat16)
            chain_copy(chunk).start()

    def columns_of(pair):
        return pl.ds(pl.multiple_of(pair * LANES, LANES), LANES)

    part = lax.broadcasted_iota(jnp.int32, (LANES, 2 * LANES), 0)
    part = (
        part
        - jnp.where(part >= heads, heads, 0)
        - jnp.where(part >= 2 * heads, heads, 0)
    )
    wide_side = lax.broadcasted_iota(jnp.int32, (LANES, 2 * LANES), 1) // LANES
    wide_index = part - wide_side
    narrow_side = lax.broadcasted_iota(jnp.int32, (LANES, LANES), 1) // HEAD_DIM
    narrow_index = part[:, 0:LANES] - narrow_side
    outside = jnp.full((LANES, LANES), -1, jnp.int32)
    block_index = jnp.concatenate(
        [
            jnp.concatenate([narrow_index, outside], axis=1),
            jnp.concatenate([outside, narrow_index], axis=1),
        ],
        axis=0,
    )
    first_half = lanes < HEAD_DIM

    def picker(index, pair):
        return jnp.where(index == 2 * pair, 1.0, 0.0).astype(jnp.bfloat16)

    def state_pair(pair):
        columns = columns_of(pair)
        both = jnp.dot(
            spread_ref[...], picker(block_index, pair), preferred_element_type=jnp.float32
        )
        own_run = both[:, 0:LANES]
        weight = both[:, LANES : 2 * LANES]
        last_run = own_run[STRETCH - 1 : STRETCH, :]
        fed = signal_ref[:, columns].astype(jnp.float32) * weight
        fed_ref[:, columns] = fed.astype(jnp.bfloat16)
        lead_ref[:, columns] = jnp.exp2(own_run)
        scaled = (fed * jnp.exp2(last_run - own_run)).astype(jnp.bfloat16)
        state_ref[pair] = jnp.dot(
            read_by_token_ref[...], scaled, preferred_element_type=jnp.float32
        )
        total_ref[pair] = jnp.broadcast_to(jnp.exp2(last_run), (8, LANES))

    def mix_pair(pair):
        columns = columns_of(pair)
        half = STRETCH // 2
        tops, bottoms = [], []
        fed = fed_ref[:, columns]
        runs = jnp.dot(
            spread_ref[:, 0:LANES], picker(wide_index, pair), preferred_element_type=jnp.float32
        )
        for side in range(2):
            row = row_ref[pl.ds(2 * pair + side, 1), :]
            run = runs[:, side * LANES : (side + 1) * LANES]
            near = jnp.exp2(jnp.minimum(run[0:half] - row[:, 0:half], 0.0))
            far = jnp.exp2(jnp.minimum(run[half:] - row[:, 0:half], 0.0))
            late = jnp.exp2(jnp.minimum(run[half:] - row[:, half:], 0.0))
            near = (near * scores_ref[0:half, 0:half]).astype(jnp.bfloat16)
            far = (far * scores_ref[half:, 0:half]).astype(jnp.bfloat16)
            late = (late * scores_ref[half:, half:]).astype(jnp.bfloat16)
            tops.append(jnp.dot(near, fed[0:half], preferred_element_type=jnp.float32))
            bottoms.append(
                jnp.dot(
                    jnp.concatenate([far, late], axis=1), fed, preferred_element_type=jnp.float32
                )
            )
        local_ref[0:half, columns] = jnp.where(first_half[0:half], tops[0], tops[1])
        local_ref[half:, columns] = jnp.where(first_half[half:], bottoms[0], bottoms[1])

    def gate_pair(chunk, member):
        pair = chunk * PAIRS + member
        columns = columns_of(pair)
        carried = jnp.dot(
            read_ref[...], carry_ref[chunk, member], preferred_element_type=jnp.float32
        )
        skip = jnp.dot(
            skip_rows_ref[...], picker(narrow_index, pair), preferred_element_type=jnp.float32
        )
        ssm_out = (
            local_ref[:, columns]
            + lead_ref[:, columns] * carried
            + skip[0:1, :] * signal_ref[:, columns].astype(jnp.float32)
        )
        gate = gate_ref[:, columns].astype(jnp.float32)
        gated = ssm_out * (gate / (1.0 + jnp.exp(-gate)))
        normed_ref[:, columns] = (gated * gain_ref[pl.ds(pair, 1), :]).astype(jnp.bfloat16)
        return gated * gated

    @pl.loop(0, pair_count // STATE_PAIRS)
    def _(group):
        for member in range(STATE_PAIRS):
            state_pair(group * STATE_PAIRS + member)

        @pl.when(place == 0)
        def _():
            for member in range(STATE_PAIRS // PAIRS):
                chain_step(group * (STATE_PAIRS // PAIRS) + member)

    delay = jnp.minimum(chunk_count, place * SLOTS)

    def chain_slot(slot):
        chunk = slot - delay

        @pl.when((place > 0) & (chunk >= 0) & (chunk < chunk_count))
        def _():
            chain_step(chunk)

    @pl.loop(0, pair_count // MIX_PAIRS)
    def _(group):
        for member in range(MIX_PAIRS // PAIRS):
            chain_slot(group * (MIX_PAIRS // PAIRS) + member)
        for member in range(MIX_PAIRS):
            mix_pair(group * MIX_PAIRS + member)

    gate_load.wait()

    @pl.loop(0, pair_count // GATE_PAIRS)
    def _(group):
        for member in range(GATE_PAIRS // PAIRS):
            chain_slot(chunk_count + group * (GATE_PAIRS // PAIRS) + member)
        squares = square_ref[...]
        for member in range(GATE_PAIRS):
            squares = squares + gate_pair(
                group * (GATE_PAIRS // PAIRS) + member // PAIRS, member % PAIRS
            )
        square_ref[...] = squares

    square_sum = jnp.sum(square_ref[...].T, axis=0, keepdims=True)
    square_out_ref[...] = jnp.broadcast_to(square_sum, square_out_ref.shape)
    square_copy = pltpu.make_async_remote_copy(
        src_ref=square_out_ref,
        dst_ref=square_in_ref,
        send_sem=square_send,
        recv_sem=square_recv,
        device_id={"tensor": peer},
        device_id_type=MESH,
    )
    square_copy.start()
    weight_load.wait()
    own_width = out_ref.shape[1]
    tile_count = own_width // TILE

    def tile_copy(tile):
        return pltpu.make_async_remote_copy(
            src_ref=sent_ref.at[tile],
            dst_ref=landed_ref.at[tile],
            send_sem=tile_send.at[tile],
            recv_sem=tile_recv.at[tile],
            device_id={"tensor": peer},
            device_id_type=MESH,
        )

    def project(owner, tile):
        start = pl.multiple_of(owner * own_width + tile * TILE, LANES)
        return jnp.dot(
            normed_ref[...], weight_ref[:, pl.ds(start, TILE)], preferred_element_type=jnp.float32
        )

    @pl.loop(0, tile_count)
    def _(tile):
        sent_ref[tile] = project(peer, tile).astype(jnp.bfloat16)
        tile_copy(tile).start()

    square_copy.wait()
    inner = 2 * heads * HEAD_DIM
    scale = lax.rsqrt((square_out_ref[0:1, :] + square_in_ref[0:1, :]) / inner + EPSILON)
    square_ref[...] = jnp.broadcast_to(scale, (LANES, STRETCH)).T

    @pl.loop(0, tile_count)
    def _(tile):
        own = project(tensor_index, tile)
        tile_copy(tile).wait_recv()
        both = own + landed_ref[tile].astype(jnp.float32)
        scales = square_ref[...]
        for side in range(TILE // LANES):
            start = pl.multiple_of(tile * TILE + side * LANES, LANES)
            out_ref[:, pl.ds(start, LANES)] = (
                both[:, side * LANES : (side + 1) * LANES] * scales
            ).astype(jnp.bfloat16)

    @pl.loop(0, tile_count)
    def _(tile):
        tile_copy(tile).wait_send()

    @pl.when(place < places - 1)
    def _():
        @pl.loop(0, chunk_count)
        def _(chunk):
            chain_copy(chunk).wait_send()


def fused_on_device(
    span_count,
    band_count,
    signal,
    gate_branch,
    write_proj,
    read_proj,
    step_logits,
    valid_mask,
    stretch_band,
    band_offset,
    decay_log,
    step_offset,
    skip_gain,
    norm_gain,
    out_weight,
):
    heads = decay_log.shape[0]
    inner = heads * HEAD_DIM
    width = out_weight.shape[1]
    pair_count = heads // 2
    chunk_count = pair_count // PAIRS
    tile_count = width // 2 // TILE
    vmem = pl.BlockSpec(memory_space=pltpu.VMEM)
    hbm = pl.BlockSpec(memory_space=pl.ANY)
    smem = pl.BlockSpec(memory_space=pltpu.SMEM)
    f32, bf16 = jnp.float32, jnp.bfloat16
    return pl.pallas_call(
        functools.partial(fused_kernel, heads, span_count, band_count),
        out_shape=pltpu.VMEM((STRETCH, width // 2), bf16),
        in_specs=[hbm, hbm] + [vmem] * 4 + [smem] + [vmem] * 5 + [hbm],
        out_specs=vmem,
        scratch_shapes=[
            pltpu.VMEM((inner, width), bf16),
            pltpu.VMEM((STRETCH, inner), bf16),
            pltpu.VMEM((STRETCH, inner), bf16),
            pltpu.VMEM((LANES, STRETCH), f32),
            pltpu.VMEM((8, LANES), f32),
            pltpu.VMEM((LANES, STRETCH), f32),
            pltpu.VMEM((STRETCH, 2 * LANES), bf16),
            pltpu.VMEM((16, LANES), bf16),
            pltpu.VMEM((STRETCH, STRETCH), f32),
            pltpu.VMEM((STATE, STRETCH), bf16),
            pltpu.VMEM((STRETCH, inner), f32),
            pltpu.VMEM((STRETCH, inner), bf16),
            pltpu.VMEM((pair_count, STATE, LANES), f32),
            pltpu.VMEM((pair_count, 8, LANES), f32),
            pltpu.VMEM((STRETCH, inner), f32),
            pltpu.VMEM((STRETCH, inner), bf16),
            pltpu.VMEM((STRETCH, LANES), f32),
            pltpu.VMEM((chunk_count, PAIRS, STATE, LANES), bf16),
            pltpu.VMEM((chunk_count, PAIRS, STATE, LANES), bf16),
            pltpu.VMEM((tile_count, STRETCH, TILE), bf16),
            pltpu.VMEM((tile_count, STRETCH, TILE), bf16),
            pltpu.VMEM((8, STRETCH), f32),
            pltpu.VMEM((8, STRETCH), f32),
            pltpu.SemaphoreType.DMA((3,)),
            pltpu.SemaphoreType.DMA((chunk_count,)),
            pltpu.SemaphoreType.DMA((chunk_count,)),
            pltpu.SemaphoreType.DMA((tile_count,)),
            pltpu.SemaphoreType.DMA((tile_count,)),
            pltpu.SemaphoreType.DMA,
            pltpu.SemaphoreType.DMA,
        ],
        compiler_params=pltpu.CompilerParams(
            collective_id=0, has_side_effects=True, vmem_limit_bytes=60 * 1024 * 1024
        ),
    )(
        signal,
        gate_branch,
        write_proj,
        read_proj,
        step_logits,
        valid_mask[None, :],
        stretch_band,
        band_offset,
        decay_log[None, :],
        step_offset[None, :],
        skip_gain[None, :],
        norm_gain.reshape(pair_count, LANES),
        out_weight,
    )


def solution(mesh):
    placed = (
        P(("group", "scan", "band"), "tensor"),
        P(("group", "scan", "band"), "tensor"),
        P(("group", "scan", "band"), None),
        P(("group", "scan", "band"), None),
        P("tensor", ("group", "scan", "band")),
        P(("group", "scan", "band")),
        P(("group", "scan", "band")),
        P(None, "tensor"),
        P("tensor"),
        P("tensor"),
        P("tensor"),
        P("tensor"),
        P("tensor", None),
    )
    shape = dict(mesh.shape)
    places = shape["scan"] * shape["band"]

    def layer(*arrays):
        rows = arrays[0].shape[0] // (shape["group"] * places)
        heads = arrays[8].shape[0] // shape["tensor"]
        width = arrays[12].shape[1]
        fits = (
            shape["tensor"] == 2
            and places > 2
            and rows == STRETCH
            and heads % (2 * STATE_PAIRS) == 0
            and heads % (2 * MIX_PAIRS) == 0
            and heads % (2 * GATE_PAIRS) == 0
            and 3 * heads <= LANES
            and width % (2 * TILE) == 0
        )
        member = on_device
        if fits:
            member = functools.partial(fused_on_device, shape["scan"], shape["band"])
        return mapped(member)(*arrays)

    def mapped(member):
        return jax.shard_map(
            member,
            mesh=mesh,
            in_specs=placed,
            out_specs=P(("group", "scan", "band"), "tensor"),
            check_vma=False,
        )

    return layer
```
